32 devices in a mesh: dp: 2 (over x), ctx: 16 (over z, y, core).
Axes of the slice: x: 2, y: 2, z: 4, core: 2. Of those that a mesh axis runs over, the one named last changes fastest.
Arguments:
- features: bfloat16 [2, 2048, 1536], P('dp', 'ctx'), may hold values from -500 to 500
- gain: float32 [1536], replicated, may hold values from 0.1 to 1.9
- conv_weight: bfloat16 [5, 1536, 768], replicated, may hold values from -0.0625 to 0.0625
- cotangent: bfloat16 [2, 2048, 768], P('dp', 'ctx'), may hold values from -15 to 15
Outputs:
- convolved: bfloat16 [2, 2048, 768], P('dp', 'ctx')
- input_grad: bfloat16 [2, 2048, 1536], P('dp', 'ctx')
- gain_grad: float32 [1536], replicated
The draws below stay inside these ranges and needn't reach their ends.
All inputs are finite; a program needn't handle non-finite values.
Results may differ from the reference program's by a relative error of at most 0.0054.
Values may be sent and summed in bfloat16 or wider, within the bound.
A program may use at most 64 MiB of HBM per device.

```python
import math
import jax
import jax.numpy as jnp
from jax import lax

CH = 1536
COUT = 768
KERNEL_TAPS = 5
LEN = 2048
DILATION_STEP = 256
BATCH = 2


def draw_features(key, part):
    first_key, second_key, third_key = jax.random.split(jax.random.fold_in(key, 11), 3)
    base = jnp.clip(jax.random.normal(first_key, (BATCH, LEN, CH), jnp.float32), -5.0, 5.0)
    row_scale = jnp.exp(jax.random.uniform(second_key, (BATCH, LEN, 1), jnp.float32, 0.0, math.log(10.0)))
    column_scale = jnp.exp(jax.random.uniform(third_key, (1, 1, CH), jnp.float32, 0.0, math.log(10.0)))
    return (base * row_scale * column_scale).astype(jnp.bfloat16)


def draw_cotangent(key, part):
    first_key = jax.random.fold_in(jax.random.fold_in(key, 23), 0)
    position = jnp.arange(LEN, dtype=jnp.float32) / max(LEN - 1, 1)
    rising = jnp.exp(math.log(3.0) * position)
    base = jnp.clip(jax.random.normal(first_key, (BATCH, LEN, COUT), jnp.float32), -5.0, 5.0)
    return (base * rising[None, :, None]).astype(jnp.bfloat16)


def noise(own_key, shape, width, most, kind=jnp.bfloat16):
    return jnp.clip(width * jax.random.normal(own_key, shape, jnp.float32), -most, most).astype(kind)


def setup_inputs(seed: int = 0) -> dict:
    key_list = jax.random.split(jax.random.key(seed), 5)
    features = draw_features(jax.random.fold_in(key_list[4], 71), 0)
    gain = jnp.clip(1.0 + 0.18 * jax.random.normal(key_list[1], (CH,), jnp.float32), 0.1, 1.9)
    conv_weight = noise(key_list[2], (KERNEL_TAPS, CH, COUT), (KERNEL_TAPS * CH) ** -0.5, 0.0625)
    cotangent = draw_cotangent(jax.random.fold_in(key_list[4], 71), 0)
    return {"features": features, "gain": gain, "conv_weight": conv_weight, "cotangent": cotangent}


EPS = 1e-06

def activate(values):
    return jax.nn.gelu(values, approximate=True)

def shifted(values, strand_heading):
    reach_length = KERNEL_TAPS // 2 * DILATION_STEP
    padded = jnp.pad(values, ((0, 0), (reach_length, reach_length), (0, 0)))
    pieces = []
    for bin_displacement in range(KERNEL_TAPS):
        start_position = reach_length + strand_heading * (bin_displacement - KERNEL_TAPS // 2) * DILATION_STEP
        pieces.append(padded[:, start_position:start_position + LEN, :])
    return pieces

def apply_forward(pieces, weight):
    lead = pieces[0].shape[0]
    middle = pieces[0].shape[1]
    total = jnp.zeros((lead * middle, weight.shape[2]), jnp.float32)
    for tap_index in range(KERNEL_TAPS):
        flat_rows = pieces[tap_index].reshape(lead * middle, pieces[tap_index].shape[2])
        total = total + jnp.dot(flat_rows, weight[tap_index], preferred_element_type=jnp.float32)
    return total.reshape(lead, middle, weight.shape[2])

def apply_backward(pieces, weight):
    lead = pieces[0].shape[0]
    middle = pieces[0].shape[1]
    total = jnp.zeros((lead * middle, weight.shape[1]), jnp.float32)
    for tap_index in range(KERNEL_TAPS):
        flat_rows = pieces[tap_index].reshape(lead * middle, pieces[tap_index].shape[2])
        total = total + lax.dot_general(flat_rows, weight[tap_index], (((1,), (1,)), ((), ())), preferred_element_type=jnp.float32)
    return total.reshape(lead, middle, weight.shape[1])

def reference(features, gain, conv_weight, cotangent):
    wide = features.astype(jnp.float32)
    inv_rms = lax.rsqrt(lax.optimization_barrier(jnp.mean(wide * wide, axis=-1, keepdims=True)) + EPS)
    normed = wide * inv_rms
    scaled = normed * gain
    hidden = activate(scaled).astype(jnp.bfloat16)
    forward_term = apply_forward(shifted(hidden, 1), conv_weight)
    turned = apply_forward(shifted(hidden[:, ::-1, ::-1], 1), conv_weight).astype(jnp.bfloat16)
    reverse_term = turned[:, ::-1, ::-1]
    convolved = (forward_term + reverse_term.astype(jnp.float32)).astype(jnp.bfloat16)
    back_forward = apply_backward(shifted(cotangent, -1), conv_weight)
    back_turned = apply_backward(shifted(cotangent[:, ::-1, ::-1], -1), conv_weight).astype(jnp.bfloat16)
    grad_hidden = back_forward + back_turned[:, ::-1, ::-1].astype(jnp.float32)
    _, pullback = jax.vjp(activate, scaled)
    grad_scaled = pullback(grad_hidden)[0]
    gain_grad = lax.optimization_barrier(jnp.sum(grad_scaled * normed, axis=(0, 1))) / math.sqrt(BATCH * LEN)
    grad_normed = grad_scaled * gain
    spread_term = lax.optimization_barrier(jnp.mean(grad_normed * normed, axis=-1, keepdims=True))
    input_grad = (inv_rms * (grad_normed - normed * spread_term)).astype(jnp.bfloat16)
    return (convolved, input_grad, gain_grad)
```

```python
import functools
import math

import jax
import jax.numpy as jnp
from jax import lax
from jax.experimental import pallas as pl
from jax.experimental.pallas import tpu as pltpu
from jax.sharding import PartitionSpec as P

TAPS = 5
MID = TAPS // 2
EPS = 1e-06
TILE = 256
CHUNK = 16
ROOT = math.sqrt(2.0 / math.pi)
CUBE = 0.044715
MESH = pl.DeviceIdType.MESH
ORDER = (0, 4, 1, 3, 2)


def body(n_dp, n_ctx, rows_total, feat, gain_ref, w, ct, conv_out, grad_out, gain_out,
         wv, xv, hh, fa, fb, csend, crecv, gg, bf, br, flip_ref, inv_ref, part, sum1, sum2,
         w_sem, x_sem, g_sem, ct_ssem, ct_rsem, c_ssem, c_rsem, s1_ssem, s1_rsem, s2_ssem, s2_rsem):
    rows, ch = xv.shape
    cout = ct.shape[-1]
    hops = n_ctx // 8
    low = 4 if n_ctx % 4 == 0 else 1
    high = n_ctx // low
    me_dp = lax.axis_index("dp")
    me = lax.axis_index("ctx")
    me_low = lax.rem(me, low)
    me_high = me // low
    group1 = n_dp * low
    slot1 = me_dp * low + me_low

    copies_w = {}
    x_copy = pltpu.make_async_copy(feat.at[0], xv, x_sem)
    x_copy.start()
    for k in ORDER:
        copies_w[k] = pltpu.make_async_copy(w.at[k], wv.at[k], w_sem.at[k])
        copies_w[k].start()
    g_copy = pltpu.make_async_copy(ct.at[0], gg.at[MID, pl.ds(0, rows)], g_sem)
    g_copy.start()

    def shifted(k):
        return me + (k - MID) * hops

    def exists(k):
        return jnp.logical_and(shifted(k) >= 0, shifted(k) < n_ctx)

    sides = [k for k in range(TAPS) if k != MID]
    far_first = (0, 4, 1, 3)

    def peer1(j):
        other = lax.rem(slot1 + j, group1)
        return {"dp": other // low, "ctx": me_high * low + lax.rem(other, low)}

    def peer2(j):
        other = lax.rem(me_high + j, high)
        return {"dp": me_dp, "ctx": other * low + me_low}

    barrier = pltpu.get_barrier_semaphore()
    count = jnp.int32(group1 - 1 + high - 1)
    for k in sides:
        @pl.when(exists(k))
        def _(k=k):
            pl.semaphore_signal(barrier, inc=1, device_id={"dp": me_dp, "ctx": shifted(k)}, device_id_type=MESH)
        count = count + exists(k).astype(jnp.int32)
    for j in range(1, group1):
        pl.semaphore_signal(barrier, inc=1, device_id=peer1(j), device_id_type=MESH)
    for j in range(1, high):
        pl.semaphore_signal(barrier, inc=1, device_id=peer2(j), device_id_type=MESH)
    pl.semaphore_wait(barrier, count)

    def ct_copy(k):
        return pltpu.make_async_remote_copy(
            src_ref=ct.at[0], dst_ref=gg.at[k, pl.ds(0, rows)],
            send_sem=ct_ssem.at[k], recv_sem=ct_rsem.at[k],
            device_id={"dp": me_dp, "ctx": shifted(k)}, device_id_type=MESH)

    def c_copy(k):
        return pltpu.make_async_remote_copy(
            src_ref=csend.at[k], dst_ref=crecv.at[k],
            send_sem=c_ssem.at[k], recv_sem=c_rsem.at[k],
            device_id={"dp": me_dp, "ctx": shifted(TAPS - 1 - k)}, device_id_type=MESH)

    for k in far_first:
        @pl.when(exists(k))
        def _(k=k):
            ct_copy(k).start()

    for k in sides:
        @pl.when(jnp.logical_not(exists(TAPS - 1 - k)))
        def _(k=k):
            gg[k, pl.ds(0, rows), :] = jnp.zeros((rows, cout), jnp.bfloat16)
        @pl.when(jnp.logical_not(exists(k)))
        def _(k=k):
            crecv[k] = jnp.zeros((rows, cout), jnp.bfloat16)

    r_iota = lax.broadcasted_iota(jnp.int32, (TILE, TILE), 0)
    c_iota = lax.broadcasted_iota(jnp.int32, (TILE, TILE), 1)
    flip_ref[...] = jnp.where(r_iota + c_iota == TILE - 1, 1.0, 0.0).astype(jnp.bfloat16)

    def flip_block(values):
        return jnp.dot(values, flip_ref[...], preferred_element_type=jnp.float32)

    def at(j):
        return pl.ds(pl.multiple_of(j * TILE, TILE), TILE)

    x_copy.wait()

    @pl.loop(0, rows // CHUNK)
    def _(i):
        here = pl.ds(pl.multiple_of(i * CHUNK, CHUNK), CHUNK)
        wide = xv[here, :].astype(jnp.float32)
        inv = lax.rsqrt(jnp.mean(wide * wide, axis=-1, keepdims=True) + EPS)
        inv_ref[here, :] = inv
        v = wide * inv * gain_ref[...]
        t = jnp.tanh(ROOT * (v + CUBE * (v * v * v)))
        hh[here, :] = (0.5 * v * (1.0 + t)).astype(jnp.bfloat16)

    @pl.loop(0, ch // TILE)
    def _(j):
        hh[pl.ds(rows, rows), at(ch // TILE - 1 - j)] = flip_block(hh[pl.ds(0, rows), at(j)]).astype(jnp.bfloat16)

    def forward(k):
        copies_w[k].wait()

        @pl.loop(0, cout // TILE)
        def _(j):
            res = jnp.dot(hh[...], wv[k, :, at(j)], preferred_element_type=jnp.float32)
            fa[k, :, at(j)] = res[:rows]
            fb[k, :, at(j)] = res[rows:].astype(jnp.bfloat16)

    def join(k):
        @pl.loop(0, cout // TILE)
        def _(j):
            csend[k, :, at(j)] = (
                fa[k, :, at(j)] + flip_block(fb[TAPS - 1 - k, :, at(cout // TILE - 1 - j)])
            ).astype(jnp.bfloat16)

        @pl.when(exists(TAPS - 1 - k))
        def _():
            c_copy(k).start()

    forward(0)
    forward(4)
    join(0)
    join(4)
    forward(1)
    forward(3)
    join(1)
    join(3)
    forward(2)

    g_copy.wait()
    for k in sides:
        @pl.when(exists(TAPS - 1 - k))
        def _(k=k):
            ct_copy(k).wait_recv()

    for k in range(TAPS):
        @pl.loop(0, cout // TILE)
        def _(j, k=k):
            gg[TAPS - 1 - k, pl.ds(rows, rows), at(cout // TILE - 1 - j)] = flip_block(
                gg[k, pl.ds(0, rows), at(j)]).astype(jnp.bfloat16)

    @pl.loop(0, ch // TILE)
    def _(j):
        total = jnp.zeros((2 * rows, TILE), jnp.float32)
        for k in range(TAPS):
            total = total + lax.dot_general(
                gg[k], wv[k, at(j), :], (((1,), (1,)), ((), ())), preferred_element_type=jnp.float32)
        bf[:, at(j)] = total[:rows]
        br[:, at(j)] = total[rows:].astype(jnp.bfloat16)

    @pl.loop(0, ch // TILE)
    def _(j):
        bf[:, at(j)] = bf[:, at(j)] + flip_block(br[:, at(ch // TILE - 1 - j)])

    part[...] = jnp.zeros_like(part)

    @pl.loop(0, rows // CHUNK)
    def _(i):
        here = pl.ds(pl.multiple_of(i * CHUNK, CHUNK), CHUNK)
        gain = gain_ref[...]
        inv = inv_ref[here, :]
        normed = xv[here, :].astype(jnp.float32) * inv
        v = normed * gain
        t = jnp.tanh(ROOT * (v + CUBE * (v * v * v)))
        slope = 0.5 * (1.0 + t) + 0.5 * v * (1.0 - t * t) * (ROOT * (1.0 + 3.0 * CUBE * (v * v)))
        product = bf[here, :] * slope
        mixed = product * normed
        part[...] += mixed[:8] + mixed[8:]
        spread = jnp.mean(mixed * gain, axis=-1, keepdims=True)
        grad_out[0, here, :] = (inv * (product * gain - normed * spread)).astype(jnp.bfloat16)

    sum1[slot1] = jnp.sum(part[...], axis=0, keepdims=True)

    def s1_copy(j):
        return pltpu.make_async_remote_copy(
            src_ref=sum1.at[slot1], dst_ref=sum1.at[slot1],
            send_sem=s1_ssem.at[j], recv_sem=s1_rsem.at[j],
            device_id=peer1(j), device_id_type=MESH)

    def s1_arrival(j):
        sender = lax.rem(slot1 + group1 - j, group1)
        return pltpu.make_async_remote_copy(
            src_ref=sum1.at[sender], dst_ref=sum1.at[sender],
            send_sem=s1_ssem.at[j], recv_sem=s1_rsem.at[j],
            device_id=peer1(j), device_id_type=MESH)

    for j in range(1, group1):
        s1_copy(j).start()
    for j in range(1, group1):
        s1_arrival(j).wait_recv()
    sum2[me_high] = jnp.sum(sum1[...], axis=0)

    def s2_copy(j):
        return pltpu.make_async_remote_copy(
            src_ref=sum2.at[me_high], dst_ref=sum2.at[me_high],
            send_sem=s2_ssem.at[j], recv_sem=s2_rsem.at[j],
            device_id=peer2(j), device_id_type=MESH)

    def s2_arrival(j):
        sender = lax.rem(me_high + high - j, high)
        return pltpu.make_async_remote_copy(
            src_ref=sum2.at[sender], dst_ref=sum2.at[sender],
            send_sem=s2_ssem.at[j], recv_sem=s2_rsem.at[j],
            device_id=peer2(j), device_id_type=MESH)

    for j in range(1, high):
        s2_copy(j).start()

    for k in sides:
        @pl.when(exists(k))
        def _(k=k):
            c_copy(k).wait_recv()

    @pl.loop(0, cout // TILE)
    def _(j):
        total = fa[MID, :, at(j)] + flip_block(fb[MID, :, at(cout // TILE - 1 - j)])
        for k in sides:
            total = total + crecv[k, :, at(j)].astype(jnp.float32)
        conv_out[0, :, at(j)] = total.astype(jnp.bfloat16)

    for j in range(1, high):
        s2_arrival(j).wait_recv()
    gain_out[...] = jnp.sum(sum2[...], axis=0) * (1.0 / math.sqrt(rows_total))

    for k in sides:
        @pl.when(exists(k))
        def _(k=k):
            ct_copy(k).wait_send()
        @pl.when(exists(TAPS - 1 - k))
        def _(k=k):
            c_copy(k).wait_send()
    for j in range(1, group1):
        s1_copy(j).wait_send()
    for j in range(1, high):
        s2_copy(j).wait_send()


def per_device(features, gain, conv_weight, cotangent):
    n_dp, n_ctx = lax.axis_size("dp"), lax.axis_size("ctx")
    lead, rows, ch = features.shape
    cout = cotangent.shape[-1]
    low = 4 if n_ctx % 4 == 0 else 1
    high = n_ctx // low
    group1 = n_dp * low
    rows_total = lead * rows * n_dp * n_ctx
    any_spec = pl.BlockSpec(memory_space=pl.ANY)
    vmem_spec = pl.BlockSpec(memory_space=pltpu.VMEM)
    bf16, f32 = jnp.bfloat16, jnp.float32
    dma = pltpu.SemaphoreType.DMA
    conv, grad, total = pl.pallas_call(
        functools.partial(body, n_dp, n_ctx, rows_total),
        out_shape=(
            jax.ShapeDtypeStruct((lead, rows, cout), bf16),
            jax.ShapeDtypeStruct((lead, rows, ch), bf16),
            jax.ShapeDtypeStruct((1, ch), f32),
        ),
        in_specs=[any_spec, vmem_spec, any_spec, any_spec],
        out_specs=(vmem_spec, vmem_spec, vmem_spec),
        scratch_shapes=[
            pltpu.VMEM((TAPS, ch, cout), bf16),
            pltpu.VMEM((rows, ch), bf16),
            pltpu.VMEM((2 * rows, ch), bf16),
            pltpu.VMEM((TAPS, rows, cout), f32),
            pltpu.VMEM((TAPS, rows, cout), bf16),
            pltpu.VMEM((TAPS, rows, cout), bf16),
            pltpu.VMEM((TAPS, rows, cout), bf16),
            pltpu.VMEM((TAPS, 2 * rows, cout), bf16),
            pltpu.VMEM((rows, ch), f32),
            pltpu.VMEM((rows, ch), bf16),
            pltpu.VMEM((TILE, TILE), bf16),
            pltpu.VMEM((rows, 1), f32),
            pltpu.VMEM((8, ch), f32),
            pltpu.VMEM((group1, 1, ch), f32),
            pltpu.VMEM((high, 1, ch), f32),
            dma((TAPS,)), dma, dma,
            dma((TAPS,)), dma((TAPS,)), dma((TAPS,)), dma((TAPS,)),
            dma((group1,)), dma((group1,)), dma((high,)), dma((high,)),
        ],
        compiler_params=pltpu.CompilerParams(
            collective_id=0, has_side_effects=True, vmem_limit_bytes=62 * 1024 * 1024),
        name="rc_block",
    )(features, gain.reshape(1, ch), conv_weight, cotangent)
    return conv, grad, total.reshape(ch)


def solution(mesh):
    return jax.shard_map(
        per_device,
        mesh=mesh,
        in_specs=(P("dp", "ctx", None), P(), P(), P("dp", "ctx", None)),
        out_specs=(P("dp", "ctx", None), P("dp", "ctx", None), P()),
        check_vma=False,
    )
```

```python
import functools
import math

import jax
import jax.numpy as jnp
from jax import lax
from jax.experimental import pallas as pl
from jax.experimental.pallas import tpu as pltpu
from jax.sharding import PartitionSpec as P

TAPS = 5
MID = TAPS // 2
EPS = 1e-06
TILE = 256
CHUNK = 16
ROOT = math.sqrt(2.0 / math.pi)
CUBE = 0.044715
MESH = pl.DeviceIdType.MESH
ORDER = (0, 4, 1, 3, 2)


def body(n_dp, n_ctx, rows_total, feat, gain_in, w, ct, conv_out, grad_out, gain_out,
         gain_ref, wv, xv, hh, fa, fb, csend, crecv, gg, bf, br, flip_ref, inv_ref, spread_ref, part, sum1, sum2,
         w_sem, x_sem, g_sem, ct_ssem, ct_rsem, c_ssem, c_rsem, s1_ssem, s1_rsem, s2_ssem, s2_rsem):
    rows, ch = xv.shape
    cout = ct.shape[-1]
    hops = n_ctx // 8
    low = 4 if n_ctx % 4 == 0 else 1
    high = n_ctx // low
    me_dp = lax.axis_index("dp")
    me = lax.axis_index("ctx")
    me_low = lax.rem(me, low)
    me_high = me // low
    group1 = n_dp * low
    slot1 = me_dp * low + me_low

    copies_w = {}
    x_copy = pltpu.make_async_copy(feat.at[0], xv, x_sem)
    x_copy.start()
    for k in ORDER:
        copies_w[k] = pltpu.make_async_copy(w.at[k], wv.at[k], w_sem.at[k])
        copies_w[k].start()
    g_copy = pltpu.make_async_copy(ct.at[0], gg.at[MID, pl.ds(0, rows)], g_sem)
    g_copy.start()

    def shifted(k):
        return me + (k - MID) * hops

    def exists(k):
        return jnp.logical_and(shifted(k) >= 0, shifted(k) < n_ctx)

    sides = [k for k in range(TAPS) if k != MID]
    far_first = (0, 4, 1, 3)

    def peer1(j):
        other = lax.rem(slot1 + j, group1)
        return {"dp": other // low, "ctx": me_high * low + lax.rem(other, low)}

    def peer2(j):
        other = lax.rem(me_high + j, high)
        return {"dp": me_dp, "ctx": other * low + me_low}

    barrier = pltpu.get_barrier_semaphore()
    count = jnp.int32(group1 - 1 + high - 1)
    for k in sides:
        @pl.when(exists(k))
        def _(k=k):
            pl.semaphore_signal(barrier, inc=1, device_id={"dp": me_dp, "ctx": shifted(k)}, device_id_type=MESH)
        count = count + exists(k).astype(jnp.int32)
    for j in range(1, group1):
        pl.semaphore_signal(barrier, inc=1, device_id=peer1(j), device_id_type=MESH)
    for j in range(1, high):
        pl.semaphore_signal(barrier, inc=1, device_id=peer2(j), device_id_type=MESH)
    pl.semaphore_wait(barrier, count)

    def ct_copy(k):
        return pltpu.make_async_remote_copy(
            src_ref=ct.at[0], dst_ref=gg.at[k, pl.ds(0, rows)],
            send_sem=ct_ssem.at[k], recv_sem=ct_rsem.at[k],
            device_id={"dp": me_dp, "ctx": shifted(k)}, device_id_type=MESH)

    def c_copy(k):
        return pltpu.make_async_remote_copy(
            src_ref=csend.at[k], dst_ref=crecv.at[k],
            send_sem=c_ssem.at[k], recv_sem=c_rsem.at[k],
            device_id={"dp": me_dp, "ctx": shifted(TAPS - 1 - k)}, device_id_type=MESH)

    for k in far_first:
        @pl.when(exists(k))
        def _(k=k):
            ct_copy(k).start()

    for k in sides:
        @pl.when(jnp.logical_not(exists(TAPS - 1 - k)))
        def _(k=k):
            gg[k, pl.ds(0, rows), :] = jnp.zeros((rows, cout), jnp.bfloat16)
        @pl.when(jnp.logical_not(exists(k)))
        def _(k=k):
            crecv[k] = jnp.zeros((rows, cout), jnp.bfloat16)

    r_iota = lax.broadcasted_iota(jnp.int32, (TILE, TILE), 0)
    c_iota = lax.broadcasted_iota(jnp.int32, (TILE, TILE), 1)
    flip_ref[...] = jnp.where(r_iota + c_iota == TILE - 1, 1.0, 0.0).astype(jnp.bfloat16)

    def flip_block(values):
        return jnp.dot(values, flip_ref[...], preferred_element_type=jnp.float32)

    def at(j):
        return pl.ds(pl.multiple_of(j * TILE, TILE), TILE)

    def flip_all(blocks):
        turned = flip_block(jnp.concatenate(blocks[::-1], axis=0))
        return [turned[n * rows:(n + 1) * rows] for n in range(len(blocks))]

    n_out, n_in = cout // TILE, ch // TILE
    top, bottom = pl.ds(0, rows), pl.ds(rows, rows)
    tile = [pl.ds(j * TILE, TILE) for j in range(max(n_out, n_in))]

    gain_ref[...] = gain_in[...].reshape(1, ch)

    x_copy.wait()

    @pl.loop(0, rows // CHUNK)
    def _(i):
        here = pl.ds(pl.multiple_of(i * CHUNK, CHUNK), CHUNK)
        wide = xv[here, :].astype(jnp.float32)
        inv = lax.rsqrt(jnp.mean(wide * wide, axis=-1, keepdims=True) + EPS)
        inv_ref[here, :] = inv
        v = wide * inv * gain_ref[...]
        t = jnp.tanh(ROOT * (v + CUBE * (v * v * v)))
        hh[here, :] = (0.5 * v * (1.0 + t)).astype(jnp.bfloat16)

    for j, block in enumerate(flip_all([hh[top, tile[j]] for j in range(n_in)])):
        hh[bottom, tile[j]] = block.astype(jnp.bfloat16)

    def forward(k):
        @pl.loop(0, cout // TILE)
        def _(j):
            res = jnp.dot(hh[...], wv[k, :, at(j)], preferred_element_type=jnp.float32)
            fa[k, :, at(j)] = res[:rows]
            fb[k, :, at(j)] = res[rows:].astype(jnp.bfloat16)

    def join(k):
        for j, block in enumerate(flip_all([fb[TAPS - 1 - k, :, tile[j]] for j in range(n_out)])):
            csend[k, :, tile[j]] = (fa[k, :, tile[j]] + block).astype(jnp.bfloat16)

        @pl.when(exists(TAPS - 1 - k))
        def _():
            c_copy(k).start()

    for k in (0, 4):
        copies_w[k].wait()
        forward(k)
    join(0)
    join(4)
    for k in (1, 3):
        copies_w[k].wait()
        forward(k)
    join(1)
    join(3)
    copies_w[MID].wait()

    g_copy.wait()
    for k in sides:
        @pl.when(exists(TAPS - 1 - k))
        def _(k=k):
            ct_copy(k).wait_recv()

    for k in range(TAPS):
        for j, block in enumerate(flip_all([gg[k, top, tile[j]] for j in range(n_out)])):
            gg[TAPS - 1 - k, bottom, tile[j]] = block.astype(jnp.bfloat16)

    @pl.loop(0, ch // TILE)
    def _(j):
        total = jnp.zeros((2 * rows, TILE), jnp.float32)
        for k in range(TAPS):
            total = total + lax.dot_general(
                gg[k], wv[k, at(j), :], (((1,), (1,)), ((), ())), preferred_element_type=jnp.float32)
        bf[:, at(j)] = total[:rows]
        br[:, at(j)] = total[rows:].astype(jnp.bfloat16)

    for j, block in enumerate(flip_all([br[:, tile[j]] for j in range(n_in)])):
        bf[:, tile[j]] = bf[:, tile[j]] + block

    part[...] = jnp.zeros_like(part)

    @pl.loop(0, rows // CHUNK)
    def _(i):
        here = pl.ds(pl.multiple_of(i * CHUNK, CHUNK), CHUNK)
        gain = gain_ref[...]
        inv = inv_ref[here, :]
        normed = xv[here, :].astype(jnp.float32) * inv
        v = normed * gain
        t = jnp.tanh(ROOT * (v + CUBE * (v * v * v)))
        slope = 0.5 * (1.0 + t) + 0.5 * v * (1.0 - t * t) * (ROOT * (1.0 + 3.0 * CUBE * (v * v)))
        product = bf[here, :] * slope
        mixed = product * normed
        part[...] += mixed[:8] + mixed[8:]
        bf[here, :] = product * gain
        spread_ref[here, :] = jnp.mean(mixed * gain, axis=-1, keepdims=True)

    sum1[slot1] = jnp.sum(part[...], axis=0, keepdims=True)

    def s1_copy(j):
        return pltpu.make_async_remote_copy(
            src_ref=sum1.at[slot1], dst_ref=sum1.at[slot1],
            send_sem=s1_ssem.at[j], recv_sem=s1_rsem.at[j],
            device_id=peer1(j), device_id_type=MESH)

    def s1_arrival(j):
        sender = lax.rem(slot1 + group1 - j, group1)
        return pltpu.make_async_remote_copy(
            src_ref=sum1.at[sender], dst_ref=sum1.at[sender],
            send_sem=s1_ssem.at[j], recv_sem=s1_rsem.at[j],
            device_id=peer1(j), device_id_type=MESH)

    for j in range(1, group1):
        s1_copy(j).start()
    forward(2)
    for j in range(1, group1):
        s1_arrival(j).wait_recv()
    sum2[me_high] = jnp.sum(sum1[...], axis=0)

    def s2_copy(j):
        return pltpu.make_async_remote_copy(
            src_ref=sum2.at[me_high], dst_ref=sum2.at[me_high],
            send_sem=s2_ssem.at[j], recv_sem=s2_rsem.at[j],
            device_id=peer2(j), device_id_type=MESH)

    def s2_arrival(j):
        sender = lax.rem(me_high + high - j, high)
        return pltpu.make_async_remote_copy(
            src_ref=sum2.at[sender], dst_ref=sum2.at[sender],
            send_sem=s2_ssem.at[j], recv_sem=s2_rsem.at[j],
            device_id=peer2(j), device_id_type=MESH)

    for j in range(1, high):
        s2_copy(j).start()

    for k in sides:
        @pl.when(exists(k))
        def _(k=k):
            c_copy(k).wait_recv()

    for j, block in enumerate(flip_all([fb[MID, :, tile[j]] for j in range(n_out)])):
        total = fa[MID, :, tile[j]] + block
        for k in sides:
            total = total + crecv[k, :, tile[j]].astype(jnp.float32)
        conv_out[0, :, tile[j]] = total.astype(jnp.bfloat16)

    @pl.loop(0, rows // CHUNK)
    def _(i):
        here = pl.ds(pl.multiple_of(i * CHUNK, CHUNK), CHUNK)
        inv = inv_ref[here, :]
        normed = xv[here, :].astype(jnp.float32) * inv
        grad_out[0, here, :] = (inv * (bf[here, :] - normed * spread_ref[here, :])).astype(jnp.bfloat16)

    for j in range(1, high):
        s2_arrival(j).wait_recv()
    gain_out[...] = jnp.sum(sum2[...], axis=0) * (1.0 / math.sqrt(rows_total))

    for k in sides:
        @pl.when(exists(k))
        def _(k=k):
            ct_copy(k).wait_send()
        @pl.when(exists(TAPS - 1 - k))
        def _(k=k):
            c_copy(k).wait_send()
    for j in range(1, group1):
        s1_copy(j).wait_send()
    for j in range(1, high):
        s2_copy(j).wait_send()


def hand_over(conv, grad, total, conv_out, grad_out, total_out):
    conv_out[...] = conv[...]
    grad_out[...] = grad[...]
    total_out[...] = total[...].reshape(total_out.shape)


def per_device(features, gain, conv_weight, cotangent):
    n_dp, n_ctx = lax.axis_size("dp"), lax.axis_size("ctx")
    lead, rows, ch = features.shape
    cout = cotangent.shape[-1]
    low = 4 if n_ctx % 4 == 0 else 1
    high = n_ctx // low
    group1 = n_dp * low
    rows_total = lead * rows * n_dp * n_ctx
    hbm_spec = pl.BlockSpec(memory_space=pltpu.HBM)
    vmem_spec = pl.BlockSpec(memory_space=pltpu.VMEM)
    bf16, f32 = jnp.bfloat16, jnp.float32
    dma = pltpu.SemaphoreType.DMA
    conv, grad, total = pl.pallas_call(
        functools.partial(body, n_dp, n_ctx, rows_total),
        out_shape=(
            jax.ShapeDtypeStruct((lead, rows, cout), bf16),
            jax.ShapeDtypeStruct((lead, rows, ch), bf16),
            jax.ShapeDtypeStruct((1, ch), f32),
        ),
        in_specs=[hbm_spec, vmem_spec, hbm_spec, hbm_spec],
        out_specs=(vmem_spec, vmem_spec, vmem_spec),
        scratch_shapes=[
            pltpu.VMEM((1, ch), f32),
            pltpu.VMEM((TAPS, ch, cout), bf16),
            pltpu.VMEM((rows, ch), bf16),
            pltpu.VMEM((2 * rows, ch), bf16),
            pltpu.VMEM((TAPS, rows, cout), f32),
            pltpu.VMEM((TAPS, rows, cout), bf16),
            pltpu.VMEM((TAPS, rows, cout), bf16),
            pltpu.VMEM((TAPS, rows, cout), bf16),
            pltpu.VMEM((TAPS, 2 * rows, cout), bf16),
            pltpu.VMEM((rows, ch), f32),
            pltpu.VMEM((rows, ch), bf16),
            pltpu.VMEM((TILE, TILE), bf16),
            pltpu.VMEM((rows, 1), f32),
            pltpu.VMEM((rows, 1), f32),
            pltpu.VMEM((8, ch), f32),
            pltpu.VMEM((group1, 1, ch), f32),
            pltpu.VMEM((high, 1, ch), f32),
            dma((TAPS,)), dma, dma,
            dma((TAPS,)), dma((TAPS,)), dma((TAPS,)), dma((TAPS,)),
            dma((group1,)), dma((group1,)), dma((high,)), dma((high,)),
        ],
        compiler_params=pltpu.CompilerParams(
            collective_id=0, has_side_effects=True, vmem_limit_bytes=53_000_000),
        name="rc_block",
    )(features, gain, conv_weight, cotangent)
    return pl.pallas_call(
        hand_over,
        out_shape=(
            jax.ShapeDtypeStruct(conv.shape, bf16),
            jax.ShapeDtypeStruct(grad.shape, bf16),
            jax.ShapeDtypeStruct((ch,), f32),
        ),
        in_specs=[vmem_spec] * 3,
        out_specs=(vmem_spec,) * 3,
        compiler_params=pltpu.CompilerParams(vmem_limit_bytes=4 * 1024 * 1024),
        name="hand_over",
    )(conv, grad, total)


def solution(mesh):
    return jax.shard_map(
        per_device,
        mesh=mesh,
        in_specs=(P("dp", "ctx", None), P(), P(), P("dp", "ctx", None)),
        out_specs=(P("dp", "ctx", None), P("dp", "ctx", None), P()),
        check_vma=False,
    )
```

```python
import functools
import math

import jax
import jax.numpy as jnp
from jax import lax
from jax.experimental import pallas as pl
from jax.experimental.pallas import tpu as pltpu
from jax.sharding import PartitionSpec as P

TAPS = 5
MID = TAPS // 2
EPS = 1e-06
TILE = 256
CHUNK = 16
ROOT = math.sqrt(2.0 / math.pi)
CUBE = 0.044715
MESH = pl.DeviceIdType.MESH
ORDER = (0, 4, 1, 3, 2)


def body(n_dp, n_ctx, rows_total, feat, gain_in, w, ct, conv_out, grad_out, gain_out,
         gain_ref, gain_v, acc, wv, xv, hh, fa, fb, csend, crecv, gg, bf, br, flip_ref, inv_ref, spread_ref, part, sum1, sum2,
         w_sem, x_sem, g_sem, v_sem, ct_ssem, ct_rsem, c_ssem, c_rsem, s1_ssem, s1_rsem, s2_ssem, s2_rsem):
    rows, ch = xv.shape
    cout = ct.shape[-1]
    hops = n_ctx // 8
    low = 4 if n_ctx % 4 == 0 else 1
    high = n_ctx // low
    me_dp = lax.axis_index("dp")
    me = lax.axis_index("ctx")
    me_low = lax.rem(me, low)
    me_high = me // low
    group1 = n_dp * low
    slot1 = me_dp * low + me_low

    copies_w = {}
    x_copy = pltpu.make_async_copy(feat.at[0], xv, x_sem)
    x_copy.start()
    v_copy = pltpu.make_async_copy(gain_in, gain_v, v_sem)
    v_copy.start()
    for k in ORDER:
        copies_w[k] = pltpu.make_async_copy(w.at[k], wv.at[k], w_sem.at[k])
        copies_w[k].start()
    g_copy = pltpu.make_async_copy(ct.at[0], gg.at[MID, pl.ds(0, rows)], g_sem)
    g_copy.start()

    def shifted(k):
        return me + (k - MID) * hops

    def exists(k):
        return jnp.logical_and(shifted(k) >= 0, shifted(k) < n_ctx)

    sides = [k for k in range(TAPS) if k != MID]
    near_first = (1, 3, 0, 4)

    def peer1(j):
        other = lax.rem(slot1 + j, group1)
        return {"dp": other // low, "ctx": me_high * low + lax.rem(other, low)}

    def peer2(j):
        other = lax.rem(me_high + j, high)
        return {"dp": me_dp, "ctx": other * low + me_low}

    barrier = pltpu.get_barrier_semaphore()
    count = jnp.int32(group1 - 1 + high - 1)
    for k in sides:
        @pl.when(exists(k))
        def _(k=k):
            pl.semaphore_signal(barrier, inc=1, device_id={"dp": me_dp, "ctx": shifted(k)}, device_id_type=MESH)
        count = count + exists(k).astype(jnp.int32)
    for j in range(1, group1):
        pl.semaphore_signal(barrier, inc=1, device_id=peer1(j), device_id_type=MESH)
    for j in range(1, high):
        pl.semaphore_signal(barrier, inc=1, device_id=peer2(j), device_id_type=MESH)
    pl.semaphore_wait(barrier, count)

    def ct_copy(k):
        return pltpu.make_async_remote_copy(
            src_ref=ct.at[0], dst_ref=gg.at[k, pl.ds(0, rows)],
            send_sem=ct_ssem.at[k], recv_sem=ct_rsem.at[k],
            device_id={"dp": me_dp, "ctx": shifted(k)}, device_id_type=MESH)

    def c_copy(k):
        return pltpu.make_async_remote_copy(
            src_ref=csend.at[k], dst_ref=crecv.at[k],
            send_sem=c_ssem.at[k], recv_sem=c_rsem.at[k],
            device_id={"dp": me_dp, "ctx": shifted(TAPS - 1 - k)}, device_id_type=MESH)

    for k in near_first:
        @pl.when(exists(k))
        def _(k=k):
            ct_copy(k).start()

    for k in sides:
        @pl.when(jnp.logical_not(exists(TAPS - 1 - k)))
        def _(k=k):
            gg[k, pl.ds(0, rows), :] = jnp.zeros((rows, cout), jnp.bfloat16)
        @pl.when(jnp.logical_not(exists(k)))
        def _(k=k):
            crecv[k] = jnp.zeros((rows, cout), jnp.bfloat16)

    r_iota = lax.broadcasted_iota(jnp.int32, (TILE, TILE), 0)
    c_iota = lax.broadcasted_iota(jnp.int32, (TILE, TILE), 1)
    flip_ref[...] = jnp.where(r_iota + c_iota == TILE - 1, 1.0, 0.0).astype(jnp.bfloat16)

    def flip_block(values):
        return jnp.dot(values, flip_ref[...], preferred_element_type=jnp.float32)

    def at(j):
        return pl.ds(pl.multiple_of(j * TILE, TILE), TILE)

    def flip_all(blocks):
        turned = flip_block(jnp.concatenate(blocks[::-1], axis=0))
        return [turned[n * rows:(n + 1) * rows] for n in range(len(blocks))]

    n_out, n_in = cout // TILE, ch // TILE
    top, bottom = pl.ds(0, rows), pl.ds(rows, rows)
    tile = [pl.ds(j * TILE, TILE) for j in range(max(n_out, n_in))]

    v_copy.wait()
    gain_ref[...] = gain_v[...].reshape(1, ch)

    x_copy.wait()

    @pl.loop(0, rows // CHUNK)
    def _(i):
        here = pl.ds(pl.multiple_of(i * CHUNK, CHUNK), CHUNK)
        wide = xv[here, :].astype(jnp.float32)
        inv = lax.rsqrt(jnp.mean(wide * wide, axis=-1, keepdims=True) + EPS)
        inv_ref[here, :] = inv
        v = wide * inv * gain_ref[...]
        t = jnp.tanh(ROOT * (v + CUBE * (v * v * v)))
        hh[here, :] = (0.5 * v * (1.0 + t)).astype(jnp.bfloat16)

    for j, block in enumerate(flip_all([hh[top, tile[j]] for j in range(n_in)])):
        hh[bottom, tile[j]] = block.astype(jnp.bfloat16)

    def forward(k):
        @pl.loop(0, cout // TILE)
        def _(j):
            res = jnp.dot(hh[...], wv[k, :, at(j)], preferred_element_type=jnp.float32)
            fa[k, :, at(j)] = res[:rows]
            fb[k, :, at(j)] = res[rows:].astype(jnp.bfloat16)

    def join(k):
        for j, block in enumerate(flip_all([fb[TAPS - 1 - k, :, tile[j]] for j in range(n_out)])):
            csend[k, :, tile[j]] = (fa[k, :, tile[j]] + block).astype(jnp.bfloat16)

    def leave(k):
        @pl.when(exists(TAPS - 1 - k))
        def _():
            c_copy(k).start()

    for k in (0, 4):
        copies_w[k].wait()
        forward(k)
    join(0)
    leave(0)
    join(4)
    leave(4)
    for k in (1, 3):
        copies_w[k].wait()
        forward(k)
    join(1)
    leave(1)
    join(3)
    copies_w[MID].wait()

    def flip_tap(k):
        for j, block in enumerate(flip_all([gg[k, top, tile[j]] for j in range(n_out)])):
            gg[TAPS - 1 - k, bottom, tile[j]] = block.astype(jnp.bfloat16)

    def backward(k, j):
        return lax.dot_general(
            gg[k], wv[k, at(j), :], (((1,), (1,)), ((), ())), preferred_element_type=jnp.float32)

    g_copy.wait()
    flip_tap(MID)

    @pl.loop(0, n_in)
    def _(j):
        acc[:, at(j)] = backward(MID, j)

    for k in sides:
        @pl.when(exists(TAPS - 1 - k))
        def _(k=k):
            ct_copy(k).wait_recv()
    for k in sides:
        flip_tap(k)

    @pl.loop(0, n_in)
    def _(j):
        total = acc[:, at(j)]
        for k in sides:
            total = total + backward(k, j)
        bf[:, at(j)] = total[:rows]
        br[:, at(j)] = total[rows:].astype(jnp.bfloat16)

    for j, block in enumerate(flip_all([br[:, tile[j]] for j in range(n_in)])):
        bf[:, tile[j]] = bf[:, tile[j]] + block

    part[...] = jnp.zeros_like(part)

    @pl.loop(0, rows // CHUNK)
    def _(i):
        here = pl.ds(pl.multiple_of(i * CHUNK, CHUNK), CHUNK)
        gain = gain_ref[...]
        inv = inv_ref[here, :]
        normed = xv[here, :].astype(jnp.float32) * inv
        v = normed * gain
        t = jnp.tanh(ROOT * (v + CUBE * (v * v * v)))
        slope = 0.5 * (1.0 + t) + 0.5 * v * (1.0 - t * t) * (ROOT * (1.0 + 3.0 * CUBE * (v * v)))
        product = bf[here, :] * slope
        mixed = product * normed
        part[...] += mixed[:8] + mixed[8:]
        bf[here, :] = product * gain
        spread_ref[here, :] = jnp.mean(mixed * gain, axis=-1, keepdims=True)

    sum1[slot1] = jnp.sum(part[...], axis=0, keepdims=True)

    def s1_copy(j):
        return pltpu.make_async_remote_copy(
            src_ref=sum1.at[slot1], dst_ref=sum1.at[slot1],
            send_sem=s1_ssem.at[j], recv_sem=s1_rsem.at[j],
            device_id=peer1(j), device_id_type=MESH)

    def s1_arrival(j):
        sender = lax.rem(slot1 + group1 - j, group1)
        return pltpu.make_async_remote_copy(
            src_ref=sum1.at[sender], dst_ref=sum1.at[sender],
            send_sem=s1_ssem.at[j], recv_sem=s1_rsem.at[j],
            device_id=peer1(j), device_id_type=MESH)

    for j in range(1, group1):
        s1_copy(j).start()
    leave(3)
    forward(2)
    for j in range(1, group1):
        s1_arrival(j).wait_recv()
    sum2[me_high] = jnp.sum(sum1[...], axis=0)

    def s2_copy(j):
        return pltpu.make_async_remote_copy(
            src_ref=sum2.at[me_high], dst_ref=sum2.at[me_high],
            send_sem=s2_ssem.at[j], recv_sem=s2_rsem.at[j],
            device_id=peer2(j), device_id_type=MESH)

    def s2_arrival(j):
        sender = lax.rem(me_high + high - j, high)
        return pltpu.make_async_remote_copy(
            src_ref=sum2.at[sender], dst_ref=sum2.at[sender],
            send_sem=s2_ssem.at[j], recv_sem=s2_rsem.at[j],
            device_id=peer2(j), device_id_type=MESH)

    for j in range(1, high):
        s2_copy(j).start()

    for k in sides:
        @pl.when(exists(k))
        def _(k=k):
            c_copy(k).wait_recv()

    for j, block in enumerate(flip_all([fb[MID, :, tile[j]] for j in range(n_out)])):
        total = fa[MID, :, tile[j]] + block
        for k in sides:
            total = total + crecv[k, :, tile[j]].astype(jnp.float32)
        conv_out[0, :, tile[j]] = total.astype(jnp.bfloat16)

    @pl.loop(0, rows // CHUNK)
    def _(i):
        here = pl.ds(pl.multiple_of(i * CHUNK, CHUNK), CHUNK)
        inv = inv_ref[here, :]
        normed = xv[here, :].astype(jnp.float32) * inv
        grad_out[0, here, :] = (inv * (bf[here, :] - normed * spread_ref[here, :])).astype(jnp.bfloat16)

    for j in range(1, high):
        s2_arrival(j).wait_recv()
    gain_out[...] = jnp.sum(sum2[...], axis=0) * (1.0 / math.sqrt(rows_total))

    for k in sides:
        @pl.when(exists(k))
        def _(k=k):
            ct_copy(k).wait_send()
        @pl.when(exists(TAPS - 1 - k))
        def _(k=k):
            c_copy(k).wait_send()
    for j in range(1, group1):
        s1_copy(j).wait_send()
    for j in range(1, high):
        s2_copy(j).wait_send()


def hand_over(conv, grad, total, conv_out, grad_out, total_out):
    conv_out[...] = conv[...]
    grad_out[...] = grad[...]
    total_out[...] = total[...].reshape(total_out.shape)


def per_device(features, gain, conv_weight, cotangent):
    n_dp, n_ctx = lax.axis_size("dp"), lax.axis_size("ctx")
    lead, rows, ch = features.shape
    cout = cotangent.shape[-1]
    low = 4 if n_ctx % 4 == 0 else 1
    high = n_ctx // low
    group1 = n_dp * low
    rows_total = lead * rows * n_dp * n_ctx
    hbm_spec = pl.BlockSpec(memory_space=pltpu.HBM)
    vmem_spec = pl.BlockSpec(memory_space=pltpu.VMEM)
    bf16, f32 = jnp.bfloat16, jnp.float32
    dma = pltpu.SemaphoreType.DMA
    conv, grad, total = pl.pallas_call(
        functools.partial(body, n_dp, n_ctx, rows_total),
        out_shape=(
            jax.ShapeDtypeStruct((lead, rows, cout), bf16),
            jax.ShapeDtypeStruct((lead, rows, ch), bf16),
            jax.ShapeDtypeStruct((1, ch), f32),
        ),
        in_specs=[hbm_spec] * 4,
        out_specs=(vmem_spec, vmem_spec, vmem_spec),
        scratch_shapes=[
            pltpu.VMEM((1, ch), f32),
            pltpu.VMEM((ch,), f32),
            pltpu.VMEM((2 * rows, ch), f32),
            pltpu.VMEM((TAPS, ch, cout), bf16),
            pltpu.VMEM((rows, ch), bf16),
            pltpu.VMEM((2 * rows, ch), bf16),
            pltpu.VMEM((TAPS, rows, cout), f32),
            pltpu.VMEM((TAPS, rows, cout), bf16),
            pltpu.VMEM((TAPS, rows, cout), bf16),
            pltpu.VMEM((TAPS, rows, cout), bf16),
            pltpu.VMEM((TAPS, 2 * rows, cout), bf16),
            pltpu.VMEM((rows, ch), f32),
            pltpu.VMEM((rows, ch), bf16),
            pltpu.VMEM((TILE, TILE), bf16),
            pltpu.VMEM((rows, 1), f32),
            pltpu.VMEM((rows, 1), f32),
            pltpu.VMEM((8, ch), f32),
            pltpu.VMEM((group1, 1, ch), f32),
            pltpu.VMEM((high, 1, ch), f32),
            dma((TAPS,)), dma, dma, dma,
            dma((TAPS,)), dma((TAPS,)), dma((TAPS,)), dma((TAPS,)),
            dma((group1,)), dma((group1,)), dma((high,)), dma((high,)),
        ],
        compiler_params=pltpu.CompilerParams(
            collective_id=0, has_side_effects=True, vmem_limit_bytes=53_000_000),
        name="rc_block",
    )(*[pltpu.with_memory_space_constraint(x, pltpu.HBM) for x in (features, gain, conv_weight, cotangent)])
    return pl.pallas_call(
        hand_over,
        out_shape=(
            jax.ShapeDtypeStruct(conv.shape, bf16),
            jax.ShapeDtypeStruct(grad.shape, bf16),
            jax.ShapeDtypeStruct((ch,), f32),
        ),
        in_specs=[vmem_spec] * 3,
        out_specs=(vmem_spec,) * 3,
        compiler_params=pltpu.CompilerParams(vmem_limit_bytes=4 * 1024 * 1024),
        name="hand_over",
    )(conv, grad, total)


def solution(mesh):
    return jax.shard_map(
        per_device,
        mesh=mesh,
        in_specs=(P("dp", "ctx", None), P(), P(), P("dp", "ctx", None)),
        out_specs=(P("dp", "ctx", None), P("dp", "ctx", None), P()),
        check_vma=False,
    )
```

```python
import functools
import math

import jax
import jax.numpy as jnp
from jax import lax
from jax.experimental import pallas as pl
from jax.experimental.pallas import tpu as pltpu
from jax.sharding import PartitionSpec as P

TAPS = 5
MID = TAPS // 2
EPS = 1e-06
TILE = 256
CHUNK = 16
ROOT = math.sqrt(2.0 / math.pi)
CUBE = 0.044715
MESH = pl.DeviceIdType.MESH
ORDER = (0, 4, 1, 3, 2)


def body(n_dp, n_ctx, rows_total, feat, gain_in, w, ct, conv_out, grad_out, gain_out,
         gain_ref, gain_v, acc, wv, xv, hh, fa, fb, csend, crecv, gg, bf, br, flip_ref, inv_ref, spread_ref, part, sum1, sum2,
         w_sem, x_sem, g_sem, v_sem, ct_ssem, ct_rsem, c_ssem, c_rsem, s1_ssem, s1_rsem, s2_ssem, s2_rsem):
    rows, ch = xv.shape
    cout = ct.shape[-1]
    hops = n_ctx // 8
    low = 4 if n_ctx % 4 == 0 else 1
    high = n_ctx // low
    me_dp = lax.axis_index("dp")
    me = lax.axis_index("ctx")
    me_low = lax.rem(me, low)
    me_high = me // low
    group1 = n_dp * low
    slot1 = me_dp * low + me_low

    copies_w = {}
    x_copy = pltpu.make_async_copy(feat.at[0], xv, x_sem)
    x_copy.start()
    v_copy = pltpu.make_async_copy(gain_in, gain_v, v_sem)
    v_copy.start()
    for k in ORDER:
        copies_w[k] = pltpu.make_async_copy(w.at[k], wv.at[k], w_sem.at[k])
        copies_w[k].start()
    g_copy = pltpu.make_async_copy(ct.at[0], gg.at[MID, pl.ds(0, rows)], g_sem)
    g_copy.start()

    def shifted(k):
        return me + (k - MID) * hops

    def exists(k):
        return jnp.logical_and(shifted(k) >= 0, shifted(k) < n_ctx)

    sides = [k for k in range(TAPS) if k != MID]
    near_first = (1, 3, 0, 4)

    def peer1(j):
        other = lax.rem(slot1 + j, group1)
        return {"dp": other // low, "ctx": me_high * low + lax.rem(other, low)}

    def peer2(j):
        other = lax.rem(me_high + j, high)
        return {"dp": me_dp, "ctx": other * low + me_low}

    barrier = pltpu.get_barrier_semaphore()
    count = jnp.int32(group1 - 1 + high - 1)
    for k in sides:
        @pl.when(exists(k))
        def _(k=k):
            pl.semaphore_signal(barrier, inc=1, device_id={"dp": me_dp, "ctx": shifted(k)}, device_id_type=MESH)
        count = count + exists(k).astype(jnp.int32)
    for j in range(1, group1):
        pl.semaphore_signal(barrier, inc=1, device_id=peer1(j), device_id_type=MESH)
    for j in range(1, high):
        pl.semaphore_signal(barrier, inc=1, device_id=peer2(j), device_id_type=MESH)
    pl.semaphore_wait(barrier, count)

    def ct_copy(k):
        return pltpu.make_async_remote_copy(
            src_ref=ct.at[0], dst_ref=gg.at[k, pl.ds(0, rows)],
            send_sem=ct_ssem.at[k], recv_sem=ct_rsem.at[k],
            device_id={"dp": me_dp, "ctx": shifted(k)}, device_id_type=MESH)

    def c_copy(k):
        return pltpu.make_async_remote_copy(
            src_ref=csend.at[k], dst_ref=crecv.at[k],
            send_sem=c_ssem.at[k], recv_sem=c_rsem.at[k],
            device_id={"dp": me_dp, "ctx": shifted(TAPS - 1 - k)}, device_id_type=MESH)

    for k in near_first:
        @pl.when(exists(k))
        def _(k=k):
            ct_copy(k).start()

    for k in sides:
        @pl.when(jnp.logical_not(exists(TAPS - 1 - k)))
        def _(k=k):
            gg[k, pl.ds(0, rows), :] = jnp.zeros((rows, cout), jnp.bfloat16)
        @pl.when(jnp.logical_not(exists(k)))
        def _(k=k):
            crecv[k] = jnp.zeros((rows, cout), jnp.bfloat16)

    r_iota = lax.broadcasted_iota(jnp.int32, (TILE, TILE), 0)
    c_iota = lax.broadcasted_iota(jnp.int32, (TILE, TILE), 1)
    flip_ref[...] = jnp.where(r_iota + c_iota == TILE - 1, 1.0, 0.0).astype(jnp.bfloat16)

    def flip_block(values):
        return jnp.dot(values, flip_ref[...], preferred_element_type=jnp.float32)

    def at(j):
        return pl.ds(pl.multiple_of(j * TILE, TILE), TILE)

    def flip_all(blocks):
        turned = flip_block(jnp.concatenate(blocks[::-1], axis=0))
        return [turned[n * rows:(n + 1) * rows] for n in range(len(blocks))]

    n_out, n_in = cout // TILE, ch // TILE
    top, bottom = pl.ds(0, rows), pl.ds(rows, rows)
    tile = [pl.ds(j * TILE, TILE) for j in range(max(n_out, n_in))]

    v_copy.wait()
    gain_ref[...] = gain_v[...].reshape(1, ch)

    x_copy.wait()

    @pl.loop(0, rows // CHUNK, unroll=2)
    def _(i):
        here = pl.ds(pl.multiple_of(i * CHUNK, CHUNK), CHUNK)
        wide = xv[here, :].astype(jnp.float32)
        inv = lax.rsqrt(jnp.mean(wide * wide, axis=-1, keepdims=True) + EPS)
        inv_ref[here, :] = inv
        v = wide * inv * gain_ref[...]
        t = jnp.tanh(ROOT * (v + CUBE * (v * v * v)))
        hh[here, :] = (0.5 * v * (1.0 + t)).astype(jnp.bfloat16)

    for j, block in enumerate(flip_all([hh[top, tile[j]] for j in range(n_in)])):
        hh[bottom, tile[j]] = block.astype(jnp.bfloat16)

    def forward(k):
        @pl.loop(0, cout // TILE, unroll=True)
        def _(j):
            res = jnp.dot(hh[...], wv[k, :, at(j)], preferred_element_type=jnp.float32)
            fa[k, :, at(j)] = res[:rows]
            fb[k, :, at(j)] = res[rows:].astype(jnp.bfloat16)

    def join(k):
        for j, block in enumerate(flip_all([fb[TAPS - 1 - k, :, tile[j]] for j in range(n_out)])):
            csend[k, :, tile[j]] = (fa[k, :, tile[j]] + block).astype(jnp.bfloat16)

    def leave(k):
        @pl.when(exists(TAPS - 1 - k))
        def _():
            c_copy(k).start()

    for k in (0, 4):
        copies_w[k].wait()
        forward(k)
    join(0)
    leave(0)
    join(4)
    leave(4)
    for k in (1, 3):
        copies_w[k].wait()
        forward(k)
    join(1)
    leave(1)
    join(3)
    copies_w[MID].wait()

    def flip_tap(k):
        for j, block in enumerate(flip_all([gg[k, top, tile[j]] for j in range(n_out)])):
            gg[TAPS - 1 - k, bottom, tile[j]] = block.astype(jnp.bfloat16)

    def backward(k, j):
        return lax.dot_general(
            gg[k], wv[k, at(j), :], (((1,), (1,)), ((), ())), preferred_element_type=jnp.float32)

    g_copy.wait()
    flip_tap(MID)

    @pl.loop(0, n_in, unroll=2)
    def _(j):
        acc[:, at(j)] = backward(MID, j)

    for k in sides:
        @pl.when(exists(TAPS - 1 - k))
        def _(k=k):
            ct_copy(k).wait_recv()
    for k in sides:
        flip_tap(k)

    @pl.loop(0, n_in, unroll=2)
    def _(j):
        total = acc[:, at(j)]
        for k in sides:
            total = total + backward(k, j)
        bf[:, at(j)] = total[:rows]
        br[:, at(j)] = total[rows:].astype(jnp.bfloat16)

    for j, block in enumerate(flip_all([br[:, tile[j]] for j in range(n_in)])):
        bf[:, tile[j]] = bf[:, tile[j]] + block

    part[...] = jnp.zeros_like(part)

    @pl.loop(0, rows // CHUNK, unroll=2)
    def _(i):
        here = pl.ds(pl.multiple_of(i * CHUNK, CHUNK), CHUNK)
        gain = gain_ref[...]
        inv = inv_ref[here, :]
        normed = xv[here, :].astype(jnp.float32) * inv
        v = normed * gain
        t = jnp.tanh(ROOT * (v + CUBE * (v * v * v)))
        slope = 0.5 * (1.0 + t) + 0.5 * v * (1.0 - t * t) * (ROOT * (1.0 + 3.0 * CUBE * (v * v)))
        product = bf[here, :] * slope
        mixed = product * normed
        part[...] += mixed[:8] + mixed[8:]
        bf[here, :] = product * gain
        spread_ref[here, :] = jnp.mean(mixed * gain, axis=-1, keepdims=True)

    sum1[slot1] = jnp.sum(part[...], axis=0, keepdims=True)

    def s1_copy(j):
        return pltpu.make_async_remote_copy(
            src_ref=sum1.at[slot1], dst_ref=sum1.at[slot1],
            send_sem=s1_ssem.at[j], recv_sem=s1_rsem.at[j],
            device_id=peer1(j), device_id_type=MESH)

    def s1_arrival(j):
        sender = lax.rem(slot1 + group1 - j, group1)
        return pltpu.make_async_remote_copy(
            src_ref=sum1.at[sender], dst_ref=sum1.at[sender],
            send_sem=s1_ssem.at[j], recv_sem=s1_rsem.at[j],
            device_id=peer1(j), device_id_type=MESH)

    for j in range(1, group1):
        s1_copy(j).start()
    leave(3)
    forward(2)
    for j in range(1, group1):
        s1_arrival(j).wait_recv()
    sum2[me_high] = jnp.sum(sum1[...], axis=0)

    def s2_copy(j):
        return pltpu.make_async_remote_copy(
            src_ref=sum2.at[me_high], dst_ref=sum2.at[me_high],
            send_sem=s2_ssem.at[j], recv_sem=s2_rsem.at[j],
            device_id=peer2(j), device_id_type=MESH)

    def s2_arrival(j):
        sender = lax.rem(me_high + high - j, high)
        return pltpu.make_async_remote_copy(
            src_ref=sum2.at[sender], dst_ref=sum2.at[sender],
            send_sem=s2_ssem.at[j], recv_sem=s2_rsem.at[j],
            device_id=peer2(j), device_id_type=MESH)

    for j in range(1, high):
        s2_copy(j).start()

    for k in sides:
        @pl.when(exists(k))
        def _(k=k):
            c_copy(k).wait_recv()

    for j, block in enumerate(flip_all([fb[MID, :, tile[j]] for j in range(n_out)])):
        total = fa[MID, :, tile[j]] + block
        for k in sides:
            total = total + crecv[k, :, tile[j]].astype(jnp.float32)
        conv_out[0, :, tile[j]] = total.astype(jnp.bfloat16)

    @pl.loop(0, rows // CHUNK, unroll=2)
    def _(i):
        here = pl.ds(pl.multiple_of(i * CHUNK, CHUNK), CHUNK)
        inv = inv_ref[here, :]
        normed = xv[here, :].astype(jnp.float32) * inv
        grad_out[0, here, :] = (inv * (bf[here, :] - normed * spread_ref[here, :])).astype(jnp.bfloat16)

    for j in range(1, high):
        s2_arrival(j).wait_recv()
    gain_out[...] = jnp.sum(sum2[...], axis=0) * (1.0 / math.sqrt(rows_total))

    for k in sides:
        @pl.when(exists(k))
        def _(k=k):
            ct_copy(k).wait_send()
        @pl.when(exists(TAPS - 1 - k))
        def _(k=k):
            c_copy(k).wait_send()
    for j in range(1, group1):
        s1_copy(j).wait_send()
    for j in range(1, high):
        s2_copy(j).wait_send()


def hand_over(conv, grad, total, conv_out, grad_out, total_out):
    conv_out[...] = conv[...]
    grad_out[...] = grad[...]
    total_out[...] = total[...].reshape(total_out.shape)


def per_device(features, gain, conv_weight, cotangent):
    n_dp, n_ctx = lax.axis_size("dp"), lax.axis_size("ctx")
    lead, rows, ch = features.shape
    cout = cotangent.shape[-1]
    low = 4 if n_ctx % 4 == 0 else 1
    high = n_ctx // low
    group1 = n_dp * low
    rows_total = lead * rows * n_dp * n_ctx
    hbm_spec = pl.BlockSpec(memory_space=pltpu.HBM)
    vmem_spec = pl.BlockSpec(memory_space=pltpu.VMEM)
    bf16, f32 = jnp.bfloat16, jnp.float32
    dma = pltpu.SemaphoreType.DMA
    conv, grad, total = pl.pallas_call(
        functools.partial(body, n_dp, n_ctx, rows_total),
        out_shape=(
            jax.ShapeDtypeStruct((lead, rows, cout), bf16),
            jax.ShapeDtypeStruct((lead, rows, ch), bf16),
            jax.ShapeDtypeStruct((1, ch), f32),
        ),
        in_specs=[hbm_spec] * 4,
        out_specs=(vmem_spec, vmem_spec, vmem_spec),
        scratch_shapes=[
            pltpu.VMEM((1, ch), f32),
            pltpu.VMEM((ch,), f32),
            pltpu.VMEM((2 * rows, ch), f32),
            pltpu.VMEM((TAPS, ch, cout), bf16),
            pltpu.VMEM((rows, ch), bf16),
            pltpu.VMEM((2 * rows, ch), bf16),
            pltpu.VMEM((TAPS, rows, cout), f32),
            pltpu.VMEM((TAPS, rows, cout), bf16),
            pltpu.VMEM((TAPS, rows, cout), bf16),
            pltpu.VMEM((TAPS, rows, cout), bf16),
            pltpu.VMEM((TAPS, 2 * rows, cout), bf16),
            pltpu.VMEM((rows, ch), f32),
            pltpu.VMEM((rows, ch), bf16),
            pltpu.VMEM((TILE, TILE), bf16),
            pltpu.VMEM((rows, 1), f32),
            pltpu.VMEM((rows, 1), f32),
            pltpu.VMEM((8, ch), f32),
            pltpu.VMEM((group1, 1, ch), f32),
            pltpu.VMEM((high, 1, ch), f32),
            dma((TAPS,)), dma, dma, dma,
            dma((TAPS,)), dma((TAPS,)), dma((TAPS,)), dma((TAPS,)),
            dma((group1,)), dma((group1,)), dma((high,)), dma((high,)),
        ],
        compiler_params=pltpu.CompilerParams(
            collective_id=0, has_side_effects=True, vmem_limit_bytes=53_000_000),
        name="rc_block",
    )(*[pltpu.with_memory_space_constraint(x, pltpu.HBM) for x in (features, gain, conv_weight, cotangent)])
    return pl.pallas_call(
        hand_over,
        out_shape=(
            jax.ShapeDtypeStruct(conv.shape, bf16),
            jax.ShapeDtypeStruct(grad.shape, bf16),
            jax.ShapeDtypeStruct((ch,), f32),
        ),
        in_specs=[vmem_spec] * 3,
        out_specs=(vmem_spec,) * 3,
        compiler_params=pltpu.CompilerParams(vmem_limit_bytes=4 * 1024 * 1024),
        name="hand_over",
    )(conv, grad, total)


def solution(mesh):
    return jax.shard_map(
        per_device,
        mesh=mesh,
        in_specs=(P("dp", "ctx", None), P(), P(), P("dp", "ctx", None)),
        out_specs=(P("dp", "ctx", None), P("dp", "ctx", None), P()),
        check_vma=False,
    )
```
